32 devices in a mesh: gx: 8 (over z, y), gy: 2 (over core), gz: 2 (over x).
Axes of the slice: x: 2, y: 2, z: 4, core: 2. Of those that a mesh axis runs over, the one named last changes fastest.
Arguments:
- populations: float32 [39, 24, 8, 256], P(None, 'gx', 'gy', 'gz'), may hold values from 0.5 to 1.5
- pore_mask: int32 [24, 8, 256], P('gx', 'gy', 'gz'), may hold values 0 or 1
Outputs:
- advanced: float32 [39, 24, 8, 256], P(None, 'gx', 'gy', 'gz')
The draws below stay inside these ranges and needn't reach their ends.
All inputs are finite; a program needn't handle non-finite values. No bound on the sum of `pore_mask` on one device may be relied on, other than what follows from the above.
Results may differ from the reference program's by a relative error of at most 0.0003.
Values sent between devices are 32-bit elements; how exact they have to be, the bound alone decides.
A program may use at most 64 MiB of HBM per device.

```python
import jax
import jax.numpy as jnp
from jax import lax

VELOCITIES = 39
STEPS = 1
NX = 24
NY = 8
NZ = 256


def touch_ends(result, own_key, smallest, top_value):
    longest = result.shape.index(max(result.shape))
    spots = []
    for shift in (0, 1):
        where = [jax.random.randint(jax.random.fold_in(own_key, axis), (), 0, length) for axis, length in enumerate(result.shape)]
        where[longest] = (where[longest] + shift) % result.shape[longest]
        spots.append(tuple(where))
    return result.at[spots[0]].set(smallest).at[spots[1]].set(top_value)


def block_levels(own_key, extent, cuts, smallest, high):
    def one(axis_at, parts):
        steps = jax.random.uniform(jax.random.fold_in(jax.random.fold_in(own_key, 6), axis_at), (parts,), jnp.float32, smallest / len(cuts), high / len(cuts))
        return jnp.repeat(jnp.exp(steps), extent[axis_at] // parts).reshape((-1,) + (1,) * (len(extent) - axis_at - 1))

    loudness = one(*cuts[0])
    for cut in cuts[1:]:
        loudness = loudness * one(*cut)
    return loudness


def setup_inputs(seed: int = 0) -> dict:
    streams_of = jax.random.split(jax.random.key(seed), 3)
    return {
        "populations": jnp.clip(0.5 + 1.0 * jax.random.uniform(streams_of[0], (VELOCITIES, NX, NY, NZ), jnp.float32) ** block_levels(streams_of[0], (VELOCITIES, NX, NY, NZ), ((1, 8), (2, 2), (3, 2)), -0.2, 0.2), 0.5, 1.5),
        "pore_mask": touch_ends((jax.random.randint(streams_of[1], (NX, NY, NZ), 0, 10) < 7).astype(jnp.int32), jax.random.fold_in(streams_of[1], 1), 0, 1),
    }


sound_sq = 2.0 / 3.0
relax_time = 0.8
pair_list = [(0, 0), (1, 1), (2, 2), (0, 1), (0, 2), (1, 2)]
triple_list = [(0, 0, 0), (1, 1, 1), (2, 2, 2), (0, 0, 1), (0, 0, 2), (1, 1, 0), (1, 1, 2), (2, 2, 0), (2, 2, 1), (0, 1, 2)]


def lattice_tables():
    shell_weights = {(0, 0, 0): 1.0 / 12.0, (0, 0, 1): 1.0 / 12.0, (1, 1, 1): 1.0 / 27.0, (0, 0, 2): 2.0 / 135.0, (0, 2, 2): 1.0 / 432.0, (0, 0, 3): 1.0 / 1620.0}
    speed_list = []
    weight_list = []
    for a in range(-3, 4):
        for b in range(-3, 4):
            for c in range(-3, 4):
                pattern = tuple(sorted((abs(a), abs(b), abs(c))))
                if pattern in shell_weights:
                    speed_list.append((a, b, c))
                    weight_list.append(shell_weights[pattern])
    count = len(speed_list)
    opposite = [speed_list.index((-v[0], -v[1], -v[2])) for v in speed_list]
    hermite = [[1.0] * count]
    scaling = [1.0]
    for a in range(3):
        hermite.append([float(v[a]) for v in speed_list])
        scaling.append(1.0 / sound_sq)
    for a, b in pair_list:
        hermite.append([float(v[a] * v[b]) - sound_sq * float(a == b) for v in speed_list])
        scaling.append((1.0 if a == b else 2.0) / (2.0 * sound_sq ** 2))
    for a, b, c in triple_list:
        hermite.append([float(v[a] * v[b] * v[c]) - sound_sq * (v[a] * float(b == c) + v[b] * float(a == c) + v[c] * float(a == b)) for v in speed_list])
        distinct = len(set((a, b, c)))
        scaling.append({1: 1.0, 2: 3.0, 3: 6.0}[distinct] / (6.0 * sound_sq ** 3))
    moment_count = len(hermite)
    project = [[hermite[j][k] * weight_list[k] for k in range(count)] for j in range(moment_count)]
    gram_matrix = [[sum(project[i][k] * hermite[j][k] for k in range(count)) for j in range(moment_count)] for i in range(moment_count)]
    hermite_t = [[hermite[j][k] for j in range(moment_count)] for k in range(count)]
    relaxing = [(1.0 - 1.0 / relax_time) * scaling[j] if j >= 4 else 0.0 for j in range(moment_count)]
    return (jnp.asarray(hermite_t, dtype=jnp.float32), jnp.asarray(project, dtype=jnp.float32), jnp.asarray(gram_matrix, dtype=jnp.float32),
            jnp.asarray(scaling, dtype=jnp.float32), jnp.asarray(relaxing, dtype=jnp.float32), speed_list, opposite)


def collide(state, pore_mask, tables):
    hermite_t, project, gram_matrix, scaling, relaxing, speeds, opposite = tables
    pop_count = state.shape[0]
    columns = state.reshape(pop_count, -1)
    moments = jnp.dot(project, columns, precision=lax.Precision.HIGHEST)
    density = moments[0]
    velocity = [moments[1 + a] / density for a in range(3)]
    pieces_list = [density] + [density * velocity[a] for a in range(3)]
    pieces_list = pieces_list + [density * velocity[a] * velocity[b] for a, b in pair_list]
    pieces_list = pieces_list + [density * velocity[a] * velocity[b] * velocity[c] for a, b, c in triple_list]
    equilibrium = scaling[:, None] * jnp.stack(pieces_list)
    excess = moments - jnp.dot(gram_matrix, equilibrium, precision=lax.Precision.HIGHEST)
    coeffs = equilibrium + relaxing[:, None] * excess
    collided = jnp.dot(hermite_t, coeffs, precision=lax.Precision.HIGHEST)
    mirrored = jnp.stack([columns[opposite[k]] for k in range(pop_count)])
    return jnp.where(pore_mask.reshape(1, -1) == 1, collided, mirrored).reshape(state.shape)


def reference(populations, pore_mask):
    tables = lattice_tables()
    speeds = tables[5]

    def collide_plane(operands):
        return collide(operands[0], operands[1], tables)

    state = populations
    for repeat in range(STEPS):
        planes = jnp.moveaxis(state, 1, 0)
        collided = lax.map(collide_plane, (planes, pore_mask))
        shifted = [jnp.roll(collided[:, k], (speeds[k][0], speeds[k][1], speeds[k][2]), axis=(0, 1, 2)) for k in range(len(speeds))]
        state = jnp.stack(shifted)
    return state
```

```python
import functools

import jax
import jax.numpy as jnp
from jax import lax
from jax.experimental import pallas as pl
from jax.experimental.pallas import tpu as pltpu
from jax.sharding import PartitionSpec as P

MESH = pl.DeviceIdType.MESH

sound_sq = 2.0 / 3.0
relax_time = 0.8
pair_list = [(0, 0), (1, 1), (2, 2), (0, 1), (0, 2), (1, 2)]
triple_list = [
    (0, 0, 0),
    (1, 1, 1),
    (2, 2, 2),
    (0, 0, 1),
    (0, 0, 2),
    (1, 1, 0),
    (1, 1, 2),
    (2, 2, 0),
    (2, 2, 1),
    (0, 1, 2),
]
shell_weights = {
    (0, 0, 0): 1.0 / 12.0,
    (0, 0, 1): 1.0 / 12.0,
    (1, 1, 1): 1.0 / 27.0,
    (0, 0, 2): 2.0 / 135.0,
    (0, 2, 2): 1.0 / 432.0,
    (0, 0, 3): 1.0 / 1620.0,
}


def lattice():
    speeds = []
    weights = []
    for a in range(-3, 4):
        for b in range(-3, 4):
            for c in range(-3, 4):
                pattern = tuple(sorted((abs(a), abs(b), abs(c))))
                if pattern in shell_weights:
                    speeds.append((a, b, c))
                    weights.append(shell_weights[pattern])
    return speeds, weights


speeds, weights = lattice()
opposite = [speeds.index((-v[0], -v[1], -v[2])) for v in speeds]


def accumulate(total, factor, term):
    if factor == 0:
        return total
    if total is None:
        return term if factor == 1 else factor * term
    if factor == 1:
        return total + term
    if factor == -1:
        return total - term
    return total + factor * term


def collide(load):
    rest = speeds.index((0, 0, 0))
    pairs = [(k, opposite[k]) for k in range(len(speeds)) if k > opposite[k]]
    density = weights[rest] * load(rest)
    first = [None] * 3
    second = {ab: None for ab in pair_list}
    third = {abc: None for abc in triple_list}
    for shell in shell_weights:
        members = [(k, o) for k, o in pairs if tuple(sorted(map(abs, speeds[k]))) == shell]
        if not members:
            continue
        part0, part1 = None, [None] * 3
        part2 = {ab: None for ab in pair_list}
        part3 = {abc: None for abc in triple_list}
        for k, o in members:
            v = speeds[k]
            even = load(k) + load(o)
            odd = load(k) - load(o)
            part0 = accumulate(part0, 1, even)
            for a, b in pair_list:
                part2[a, b] = accumulate(part2[a, b], v[a] * v[b], even)
            for a in range(3):
                part1[a] = accumulate(part1[a], v[a], odd)
            for a, b, c in triple_list:
                part3[a, b, c] = accumulate(part3[a, b, c], v[a] * v[b] * v[c], odd)
        w = shell_weights[shell]
        density = accumulate(density, w, part0)
        for a in range(3):
            first[a] = accumulate(first[a], w, part1[a])
        for ab in pair_list:
            if part2[ab] is not None:
                second[ab] = accumulate(second[ab], w, part2[ab])
        for abc in triple_list:
            if part3[abc] is not None:
                third[abc] = accumulate(third[abc], w, part3[abc])

    inverse = 1.0 / density
    u = [first[a] * inverse for a in range(3)]
    relax = 1.0 - 1.0 / relax_time
    const = density
    linear = [first[a] * (1.0 / sound_sq) for a in range(3)]
    quad, cubic = {}, {}
    flux = {}
    for a, b in pair_list:
        flux[a, b] = first[a] * u[b]
        moment = second[a, b]
        if a == b:
            moment = moment - sound_sq * density
        scale = (1.0 if a == b else 2.0) / (2.0 * sound_sq**2)
        quad[a, b] = (scale * (1.0 - relax)) * flux[a, b] + (scale * relax) * moment
        if a == b:
            const = const - sound_sq * quad[a, b]
    for a, b, c in triple_list:
        moment = third[a, b, c]
        if a == b == c:
            moment = moment - (3.0 * sound_sq) * first[a]
        elif a == b:
            moment = moment - sound_sq * first[c]
        pair = (a, b) if (a, b) in flux else (b, a)
        scale = {1: 1.0, 2: 3.0, 3: 6.0}[len({a, b, c})] / (6.0 * sound_sq**3)
        cubic[a, b, c] = (scale * (1.0 - relax)) * (flux[pair] * u[c]) + (scale * relax) * moment
        if a == b == c:
            linear[a] = linear[a] - (3.0 * sound_sq) * cubic[a, b, c]
        elif a == b:
            linear[c] = linear[c] - sound_sq * cubic[a, b, c]

    return const, linear, quad, cubic


def half_sums(coefficients, k):
    const, linear, quad, cubic = coefficients
    v = speeds[k]
    even, odd = const, None
    for a, b in pair_list:
        even = accumulate(even, float(v[a] * v[b]), quad[a, b])
    for a in range(3):
        odd = accumulate(odd, float(v[a]), linear[a])
    for a, b, c in triple_list:
        odd = accumulate(odd, float(v[a] * v[b] * v[c]), cubic[a, b, c])
    return even, odd


def collided(load, pore, coefficients, k):
    o = opposite[k]
    if k == o:
        return jnp.where(pore, coefficients[0], load(o))
    even, odd = half_sums(coefficients, max(k, o))
    return jnp.where(pore, even + odd if k > o else even - odd, load(o))


def cut(speed, extent):
    if speed >= 0:
        return (0, extent - speed), (speed, extent), (extent - speed, extent), (0, speed)
    return (-speed, extent), (0, extent + speed), (0, -speed), (extent + speed, extent)


def merge_key(speed, rows, extent):
    return abs(speed) if 2 * rows <= extent else speed


def make_plan(nx, ny):
    sizes, slots, pieces = {}, {}, []
    for k, (cx, cy, cz) in enumerate(speeds):
        stay_from, stay_to, leave_from, leave_to = cut(cx, nx)
        own = []
        for source, land, dx in ((stay_from, stay_to, 0), (leave_from, leave_to, (cx > 0) - (cx < 0))):
            count = source[1] - source[0]
            if count == 0:
                continue
            where = {}
            for oy in (0, 1):
                for oz in (0, 1):
                    if (oy and not cy) or (oz and not cz) or (dx, oy, oz) == (0, 0, 0):
                        continue
                    key = (
                        dx,
                        oy,
                        oz,
                        cx,
                        merge_key(cy, abs(cy) if oy else ny - abs(cy), ny),
                        abs(cz) if oz else cz,
                    )
                    if key not in slots:
                        slots[key] = sizes.get((dx, oy, oz), 0)
                        sizes[dx, oy, oz] = slots[key] + count
                    where[oy, oz] = slots[key]
            own.append((source, land, dx, where))
        pieces.append(own)
    return sizes, pieces


def neighbours(count):
    return (1,) if count == 2 else (1, -1)


def step_kernel(counts, sizes, pieces, messages, names, pop_hbm, mask_hbm, out_ref, *scratch):
    nx, ny, nz = out_ref.shape[1:]
    *scratch, pop_ref, mask_ref, load_sem, near_sem = scratch
    send = dict(zip(names, scratch[: len(names)]))
    recv = dict(zip(messages, scratch[len(names) : len(names) + len(messages)]))
    send_sem, recv_sem = scratch[len(names) + len(messages) :]
    loads = [
        pltpu.make_async_copy(pop_hbm, pop_ref, load_sem.at[0]),
        pltpu.make_async_copy(mask_hbm, mask_ref, load_sem.at[1]),
    ]
    for load in loads:
        load.start()
    here = [lax.axis_index(axis) for axis in ("gx", "gy", "gz")]
    gx, length = here[0], counts[0]
    first, last = gx == 0, gx == length - 1
    inner = (gx > 0) & (gx < length - 1)

    def target(step):
        return {
            axis: lax.rem(at + (s + count), count)
            for axis, at, s, count in zip(("gx", "gy", "gz"), here, step, counts)
            if s
        }

    group = {dx: [step for step in messages if step[0] == dx] for dx in (1, -1, 0)}
    barrier = pltpu.get_barrier_semaphore()

    def greet(dx):
        for step in group[dx]:
            pl.semaphore_signal(barrier, inc=1, device_id=target(step), device_id_type=MESH)

    pl.when(gx != length - 2)(lambda: greet(1))
    pl.when(gx != 1)(lambda: greet(-1))
    pl.when(inner)(lambda: greet(0))

    copies = {}
    for number, step in enumerate(messages):
        kind = (step[0], abs(step[1]), abs(step[2]))
        copies[step] = pltpu.make_async_remote_copy(
            src_ref=send[kind],
            dst_ref=recv[step],
            send_sem=send_sem.at[number],
            recv_sem=recv_sem.at[number],
            device_id=target(step),
            device_id_type=MESH,
        )

    def depart(dx):
        for step in group[dx]:
            copies[step].start()

    for load in loads:
        load.wait()

    every_lane = slice(0, nz)
    loaders = [lambda j, row=row: pop_ref[j, row] for row in range(nx)]
    pores = [mask_ref[row] == 1 for row in range(nx)]
    coefficients = {}

    def place(k, row):
        if row not in coefficients:
            coefficients[row] = collide(loaders[row])
        cx, cy, cz = speeds[k]
        plane = collided(loaders[row], pores[row], coefficients[row], k)
        if cz:
            plane = pltpu.roll(plane, cz % nz, 1)
        y_stay, y_land, y_leave, y_wrap = (slice(*span) for span in cut(cy, ny))
        z_wrap = slice(*cut(cz, nz)[3])
        for source, land, dx, where in pieces[k]:
            if not source[0] <= row < source[1]:
                continue
            at = row - source[0]
            kept = plane[y_stay]
            if dx == 0:
                out_ref[k, land[0] + at, y_land, every_lane] = kept
            else:
                send[dx, 0, 0][where[0, 0] + at, y_land, every_lane] = kept
            if cy:
                moved = plane[y_leave]
                send[dx, 1, 0][where[1, 0] + at, y_wrap, every_lane] = moved
            if cz:
                send[dx, 0, 1][where[0, 1] + at, y_land, z_wrap] = kept[:, z_wrap]
            if cy and cz:
                send[dx, 1, 1][where[1, 1] + at, y_wrap, z_wrap] = moved[:, z_wrap]

    def place_all(dx):
        for row in reversed(range(nx)) if dx > 0 else range(nx):
            for k, (cx, _, _) in enumerate(speeds):
                to = row + cx
                if (to >= nx) - (to < 0) == dx:
                    place(k, row)

    place_all(1)
    pl.when(inner)(lambda: pl.semaphore_wait(barrier, len(messages)))
    pl.when(last)(lambda: pl.semaphore_wait(barrier, len(group[1])))

    def tell(dx):
        for step in group[dx]:
            pl.semaphore_signal(near_sem, inc=1, device_id=target(step), device_id_type=MESH)

    pl.when(gx == 1)(lambda: tell(-1))
    pl.when(gx == length - 2)(lambda: tell(1))
    pl.when(first)(lambda: pl.semaphore_wait(near_sem, len(group[1])))
    depart(1)
    place_all(-1)
    pl.when(inner)(lambda: depart(-1))
    place_all(0)
    pl.when(last)(lambda: pl.semaphore_wait(near_sem, len(group[-1])))
    depart(0)
    pl.when(last)(lambda: depart(-1))

    @pl.when(first)
    def _():
        pl.semaphore_wait(barrier, len(group[-1]))
        depart(-1)

    def came_by(step, speed):
        return step == 0 or step * speed > 0

    def block(span, rows, lanes):
        return (slice(*span), slice(*rows), slice(*lanes))

    for step in group[0] + group[-1][::-1] + group[1][::-1]:
        copies[step].wait_recv()
        got = recv[step]
        dx, sy, sz = step
        for k, (cx, cy, cz) in enumerate(speeds):
            if (sy and not cy) or (sz and not cz):
                continue
            if counts[1] != 2 and not came_by(sy, cy):
                continue
            if counts[2] != 2 and not came_by(sz, cz):
                continue
            _, y_land, _, y_wrap = cut(cy, ny)
            rows = y_wrap if sy else y_land
            lanes = cut(cz, nz)[3 if sz else 1]
            for source, land, piece_dx, where in pieces[k]:
                if piece_dx != dx:
                    continue
                at = where[abs(sy), abs(sz)]
                span = (at, at + source[1] - source[0])
                out_ref[(k,) + block(land, rows, lanes)] = got[block(span, rows, lanes)]
    for step in messages:
        copies[step].wait_send()


def body(counts, populations, pore_mask):
    nx, ny, nz = populations.shape[1:]
    sizes, pieces = make_plan(nx, ny)
    names = sorted(sizes)
    messages = []
    for dx, oy, oz in [(dx, oy, oz) for dx in (1, -1) for oz, oy in ((1, 0), (1, 1), (0, 0), (0, 1))] + [
        (0, 0, 1),
        (0, 1, 0),
        (0, 1, 1),
    ]:
        for sy in neighbours(counts[1]) if oy else (0,):
            for sz in neighbours(counts[2]) if oz else (0,):
                messages.append((dx, sy, sz))
    kernel = functools.partial(step_kernel, counts, sizes, pieces, messages, names)
    shape = lambda name: pltpu.VMEM((sizes[name[0], abs(name[1]), abs(name[2])], ny, nz), jnp.float32)
    return pl.pallas_call(
        kernel,
        out_shape=pltpu.VMEM(populations.shape, populations.dtype),
        in_specs=[pl.BlockSpec(memory_space=pl.ANY)] * 2,
        out_specs=pl.BlockSpec(memory_space=pltpu.VMEM),
        scratch_shapes=[shape(name) for name in names]
        + [shape(step) for step in messages]
        + [pltpu.SemaphoreType.DMA((len(messages),)), pltpu.SemaphoreType.DMA((len(messages),))]
        + [
            pltpu.VMEM(populations.shape, populations.dtype),
            pltpu.VMEM(pore_mask.shape, pore_mask.dtype),
            pltpu.SemaphoreType.DMA((2,)),
            pltpu.SemaphoreType.REGULAR,
        ],
        compiler_params=pltpu.CompilerParams(collective_id=0, has_side_effects=True),
    )(populations, pore_mask)


def solution(mesh):
    counts = tuple(mesh.shape[axis] for axis in ("gx", "gy", "gz"))
    placed = (P(None, "gx", "gy", "gz"), P("gx", "gy", "gz"))
    return jax.shard_map(
        functools.partial(body, counts),
        mesh=mesh,
        in_specs=placed,
        out_specs=P(None, "gx", "gy", "gz"),
        check_vma=False,
    )
```

```python
import functools

import jax
import jax.numpy as jnp
from jax import lax
from jax.experimental import pallas as pl
from jax.experimental.pallas import tpu as pltpu
from jax.sharding import PartitionSpec as P

MESH = pl.DeviceIdType.MESH

sound_sq = 2.0 / 3.0
relax_time = 0.8
pair_list = [(0, 0), (1, 1), (2, 2), (0, 1), (0, 2), (1, 2)]
triple_list = [
    (0, 0, 0),
    (1, 1, 1),
    (2, 2, 2),
    (0, 0, 1),
    (0, 0, 2),
    (1, 1, 0),
    (1, 1, 2),
    (2, 2, 0),
    (2, 2, 1),
    (0, 1, 2),
]
shell_weights = {
    (0, 0, 0): 1.0 / 12.0,
    (0, 0, 1): 1.0 / 12.0,
    (1, 1, 1): 1.0 / 27.0,
    (0, 0, 2): 2.0 / 135.0,
    (0, 2, 2): 1.0 / 432.0,
    (0, 0, 3): 1.0 / 1620.0,
}


def lattice():
    speeds = []
    weights = []
    for a in range(-3, 4):
        for b in range(-3, 4):
            for c in range(-3, 4):
                pattern = tuple(sorted((abs(a), abs(b), abs(c))))
                if pattern in shell_weights:
                    speeds.append((a, b, c))
                    weights.append(shell_weights[pattern])
    return speeds, weights


speeds, weights = lattice()
opposite = [speeds.index((-v[0], -v[1], -v[2])) for v in speeds]


def accumulate(total, factor, term):
    if factor == 0:
        return total
    if total is None:
        return term if factor == 1 else factor * term
    if factor == 1:
        return total + term
    if factor == -1:
        return total - term
    return total + factor * term


def collide(load):
    rest = speeds.index((0, 0, 0))
    pairs = [(k, opposite[k]) for k in range(len(speeds)) if k > opposite[k]]
    density = weights[rest] * load(rest)
    first = [None] * 3
    second = {ab: None for ab in pair_list}
    third = {abc: None for abc in triple_list}
    for shell in shell_weights:
        members = [(k, o) for k, o in pairs if tuple(sorted(map(abs, speeds[k]))) == shell]
        if not members:
            continue
        part0, part1 = None, [None] * 3
        part2 = {ab: None for ab in pair_list}
        part3 = {abc: None for abc in triple_list}
        for k, o in members:
            v = speeds[k]
            even = load(k) + load(o)
            odd = load(k) - load(o)
            part0 = accumulate(part0, 1, even)
            for a, b in pair_list:
                part2[a, b] = accumulate(part2[a, b], v[a] * v[b], even)
            for a in range(3):
                part1[a] = accumulate(part1[a], v[a], odd)
            for a, b, c in triple_list:
                part3[a, b, c] = accumulate(part3[a, b, c], v[a] * v[b] * v[c], odd)
        w = shell_weights[shell]
        density = accumulate(density, w, part0)
        for a in range(3):
            first[a] = accumulate(first[a], w, part1[a])
        for ab in pair_list:
            if part2[ab] is not None:
                second[ab] = accumulate(second[ab], w, part2[ab])
        for abc in triple_list:
            if part3[abc] is not None:
                third[abc] = accumulate(third[abc], w, part3[abc])

    inverse = 1.0 / density
    u = [first[a] * inverse for a in range(3)]
    relax = 1.0 - 1.0 / relax_time
    const = density
    linear = [first[a] * (1.0 / sound_sq) for a in range(3)]
    quad, cubic = {}, {}
    flux = {}
    for a, b in pair_list:
        flux[a, b] = first[a] * u[b]
        moment = second[a, b]
        if a == b:
            moment = moment - sound_sq * density
        scale = (1.0 if a == b else 2.0) / (2.0 * sound_sq**2)
        quad[a, b] = (scale * (1.0 - relax)) * flux[a, b] + (scale * relax) * moment
        if a == b:
            const = const - sound_sq * quad[a, b]
    for a, b, c in triple_list:
        moment = third[a, b, c]
        if a == b == c:
            moment = moment - (3.0 * sound_sq) * first[a]
        elif a == b:
            moment = moment - sound_sq * first[c]
        pair = (a, b) if (a, b) in flux else (b, a)
        scale = {1: 1.0, 2: 3.0, 3: 6.0}[len({a, b, c})] / (6.0 * sound_sq**3)
        cubic[a, b, c] = (scale * (1.0 - relax)) * (flux[pair] * u[c]) + (scale * relax) * moment
        if a == b == c:
            linear[a] = linear[a] - (3.0 * sound_sq) * cubic[a, b, c]
        elif a == b:
            linear[c] = linear[c] - sound_sq * cubic[a, b, c]

    return const, linear, quad, cubic


def half_sums(coefficients, k):
    const, linear, quad, cubic = coefficients
    v = speeds[k]
    even, odd = const, None
    for a, b in pair_list:
        even = accumulate(even, float(v[a] * v[b]), quad[a, b])
    for a in range(3):
        odd = accumulate(odd, float(v[a]), linear[a])
    for a, b, c in triple_list:
        odd = accumulate(odd, float(v[a] * v[b] * v[c]), cubic[a, b, c])
    return even, odd


def collided(load, pore, coefficients, k):
    o = opposite[k]
    if k == o:
        return jnp.where(pore, coefficients[0], load(o))
    even, odd = half_sums(coefficients, max(k, o))
    return jnp.where(pore, even + odd if k > o else even - odd, load(o))


def cut(speed, extent):
    if speed >= 0:
        return (0, extent - speed), (speed, extent), (extent - speed, extent), (0, speed)
    return (-speed, extent), (0, extent + speed), (0, -speed), (extent + speed, extent)


def merge_key(speed, rows, extent):
    return abs(speed) if 2 * rows <= extent else speed


def make_plan(nx, ny):
    sizes, slots, pieces = {}, {}, []
    for k, (cx, cy, cz) in enumerate(speeds):
        stay_from, stay_to, leave_from, leave_to = cut(cx, nx)
        own = []
        for source, land, dx in ((stay_from, stay_to, 0), (leave_from, leave_to, (cx > 0) - (cx < 0))):
            count = source[1] - source[0]
            if count == 0:
                continue
            where = {}
            for oy in (0, 1):
                for oz in (0, 1):
                    if (oy and not cy) or (oz and not cz) or (dx, oy, oz) == (0, 0, 0):
                        continue
                    key = (
                        dx,
                        oy,
                        oz,
                        cx,
                        merge_key(cy, abs(cy) if oy else ny - abs(cy), ny),
                        abs(cz) if oz else cz,
                    )
                    if key not in slots:
                        slots[key] = sizes.get((dx, oy, oz), 0)
                        sizes[dx, oy, oz] = slots[key] + count
                    where[oy, oz] = slots[key]
            own.append((source, land, dx, where))
        pieces.append(own)
    return sizes, pieces


def kind_of(step):
    return step[0], abs(step[1]), abs(step[2])


def neighbours(count):
    return (1,) if count == 2 else (1, -1)


def step_kernel(counts, pieces, messages, leave, arrive, pop_hbm, mask_hbm, out_ref, *scratch):
    send_ref, recv_ref, handed_ref, pop_ref, mask_ref = scratch[:5]
    send_sem, recv_sem, near_sem, handed_sem, forward_sem = scratch[5:]
    nx, ny, nz = out_ref.shape[1:]
    loads = [
        pltpu.make_async_copy(pop_hbm, pop_ref, send_sem.at[0]),
        pltpu.make_async_copy(mask_hbm, mask_ref, send_sem.at[1]),
    ]
    for load in loads:
        load.start()
    here = [lax.axis_index(axis) for axis in ("gx", "gy", "gz")]
    gx, length = here[0], counts[0]
    relay = length // 2
    first, last = gx == 0, gx == length - 1
    inner = (gx > 0) & (gx < length - 1)

    def target(step):
        return {
            axis: lax.rem(at + (s + count), count)
            for axis, at, s, count in zip(("gx", "gy", "gz"), here, step, counts)
            if s
        }

    def at_gx(step, index):
        return {**target((0,) + step[1:]), "gx": index}

    group = {dx: [step for step in messages if step[0] == dx] for dx in (1, 0, -1)}
    barrier = pltpu.get_barrier_semaphore()

    def signal(semaphore, device):
        pl.semaphore_signal(semaphore, inc=1, device_id=device, device_id_type=MESH)

    def greet(dx):
        for step in group[dx]:
            signal(barrier, target(step))

    greet(-1)
    pl.when(gx < length - 2)(lambda: greet(1))
    pl.when(gx < length - 1)(lambda: greet(0))

    @pl.when(last)
    def _():
        for step in group[-1]:
            signal(barrier, at_gx(step, relay))

    pl.when(gx == relay)(lambda: signal(barrier, {"gx": 0}))

    def remote(source, landing, send_semaphore, recv_semaphore, device):
        return pltpu.make_async_remote_copy(
            src_ref=source,
            dst_ref=landing,
            send_sem=send_semaphore,
            recv_sem=recv_semaphore,
            device_id=device,
            device_id_type=MESH,
        )

    def rows_of(ref, spans):
        spans = list(spans)
        return ref.at[pl.ds(spans[0][0], spans[-1][1] - spans[0][0])]

    def await_bytes(semaphore, ref):
        pltpu.make_async_copy(ref, ref, semaphore).wait()

    received = {dx: rows_of(recv_ref, (arrive[step] for step in group[dx])) for dx in group}
    arrival_sem = {dx: recv_sem.at[number] for number, dx in enumerate(group)}
    away_sem = {1: send_sem.at[0], 0: send_sem.at[0], -1: send_sem.at[1]}
    first_handed = min(span[0] for name, span in leave.items() if name[0] == -1)
    to_hand = rows_of(send_ref, (leave[name] for name in leave if name[0] == -1))
    hand = remote(to_hand, handed_ref, send_sem.at[1], handed_sem, {"gx": relay})

    def depart(steps):
        for step in steps:
            remote(
                rows_of(send_ref, [leave[kind_of(step)]]),
                rows_of(recv_ref, [arrive[step]]),
                away_sem[step[0]],
                arrival_sem[step[0]],
                target(step),
            ).start()

    def forward(steps):
        for step in steps:
            start, stop = leave[kind_of(step)]
            remote(
                rows_of(handed_ref, [(start - first_handed, stop - first_handed)]),
                rows_of(recv_ref, [arrive[step]]),
                forward_sem,
                arrival_sem[step[0]],
                at_gx(step, length - 1),
            ).start()

    for load in loads:
        load.wait()

    every_lane = slice(0, nz)
    loaders = [lambda j, row=row: pop_ref[j, row] for row in range(nx)]
    pores = [mask_ref[row] == 1 for row in range(nx)]
    coefficients = {}

    def place(k, row):
        if row not in coefficients:
            coefficients[row] = collide(loaders[row])
        cx, cy, cz = speeds[k]
        plane = collided(loaders[row], pores[row], coefficients[row], k)
        if cz:
            plane = pltpu.roll(plane, cz % nz, 1)
        y_stay, y_land, y_leave, y_wrap = (slice(*span) for span in cut(cy, ny))
        z_wrap = slice(*cut(cz, nz)[3])
        for source, land, dx, where in pieces[k]:
            if not source[0] <= row < source[1]:
                continue
            at = row - source[0]

            def slot(oy, oz):
                return leave[dx, oy, oz][0] + where[oy, oz] + at

            kept = plane[y_stay]
            if dx == 0:
                out_ref[k, land[0] + at, y_land, every_lane] = kept
            else:
                send_ref[slot(0, 0), y_land, every_lane] = kept
            if cy:
                moved = plane[y_leave]
                send_ref[slot(1, 0), y_wrap, every_lane] = moved
            if cz:
                send_ref[slot(0, 1), y_land, z_wrap] = kept[:, z_wrap]
            if cy and cz:
                send_ref[slot(1, 1), y_wrap, z_wrap] = moved[:, z_wrap]

    def place_all(dx, chosen=lambda cz: True):
        for row in reversed(range(nx)) if dx > 0 else range(nx):
            for k, (cx, _, cz) in enumerate(speeds):
                to = row + cx
                if (to >= nx) - (to < 0) == dx and chosen(cz):
                    place(k, row)

    at_first, at_last, at_relay = (jnp.where(gx == at, 1, 0) for at in (0, length - 1, relay))
    heard = len(messages) + at_relay * len(group[-1])
    heard -= at_first * (len(group[-1]) - 1) + at_last * (len(messages) - len(group[1]))
    place_all(1, lambda cz: cz != 0)
    pl.semaphore_wait(barrier, heard)
    depart([step for step in group[1] if step[2]])

    @pl.when(gx == length - 2)
    def _():
        for step in group[1]:
            signal(near_sem, target(step))

    place_all(1, lambda cz: cz == 0)
    place_all(-1)
    place_all(0)
    depart([step for step in group[1] if not step[2]])
    pl.when(first)(lambda: hand.start())
    pl.when(inner)(lambda: depart(group[-1]))
    pl.when(last)(lambda: pl.semaphore_wait(near_sem, len(group[-1])))
    depart(group[0])
    pl.when(last)(lambda: depart(group[-1]))

    @pl.when(gx == relay)
    def _():
        hand.wait_recv()
        forward(group[-1])

    def came_by(step, speed):
        return step == 0 or step * speed > 0

    def block(span, rows, lanes):
        return (slice(*span), slice(*rows), slice(*lanes))

    def unpack(dx):
        await_bytes(arrival_sem[dx], received[dx])
        for step in group[dx]:
            _, sy, sz = step
            for k, (cx, cy, cz) in enumerate(speeds):
                if (sy and not cy) or (sz and not cz):
                    continue
                if counts[1] != 2 and not came_by(sy, cy):
                    continue
                if counts[2] != 2 and not came_by(sz, cz):
                    continue
                _, y_land, _, y_wrap = cut(cy, ny)
                rows = y_wrap if sy else y_land
                lanes = cut(cz, nz)[3 if sz else 1]
                for source, land, piece_dx, where in pieces[k]:
                    if piece_dx != dx:
                        continue
                    at = arrive[step][0] + where[abs(sy), abs(sz)]
                    span = (at, at + source[1] - source[0])
                    out_ref[(k,) + block(land, rows, lanes)] = recv_ref[block(span, rows, lanes)]

    unpack(0)
    unpack(-1)
    await_bytes(send_sem.at[0], rows_of(recv_ref, (arrive[step] for step in group[1] + group[0])))
    pl.when(first)(lambda: hand.wait_send())
    pl.when(gx > 0)(lambda: await_bytes(send_sem.at[1], received[-1]))
    pl.when(gx == relay)(lambda: await_bytes(forward_sem, received[-1]))
    unpack(1)


def lay_out(keys, size):
    spans, start = {}, 0
    for key in keys:
        spans[key] = (start, start + size(key))
        start += size(key)
    return spans, start


def body(counts, populations, pore_mask):
    nx, ny = populations.shape[1:3]
    sizes, pieces = make_plan(nx, ny)
    messages = []
    for dx, oz, oy in [(dx, oz, oy) for dx in (1, 0, -1) for oz, oy in ((1, 0), (1, 1), (0, 0), (0, 1))]:
        if (dx, oz, oy) == (0, 0, 0):
            continue
        for sy in neighbours(counts[1]) if oy else (0,):
            for sz in neighbours(counts[2]) if oz else (0,):
                messages.append((dx, sy, sz))
    kinds = list(dict.fromkeys(kind_of(step) for step in messages))
    leave, leaving = lay_out(kinds, lambda kind: sizes[kind])
    arrive, arriving = lay_out(messages, lambda step: sizes[kind_of(step)])
    handed = sum(sizes[kind] for kind in kinds if kind[0] == -1)
    rows = lambda count: pltpu.VMEM((count, ny, populations.shape[3]), jnp.float32)
    return pl.pallas_call(
        functools.partial(step_kernel, counts, pieces, messages, leave, arrive),
        out_shape=pltpu.VMEM(populations.shape, populations.dtype),
        in_specs=[pl.BlockSpec(memory_space=pl.ANY)] * 2,
        out_specs=pl.BlockSpec(memory_space=pltpu.VMEM),
        scratch_shapes=[
            rows(leaving),
            rows(arriving),
            rows(handed),
            pltpu.VMEM(populations.shape, populations.dtype),
            pltpu.VMEM(pore_mask.shape, pore_mask.dtype),
            pltpu.SemaphoreType.DMA((2,)),
            pltpu.SemaphoreType.DMA((3,)),
            pltpu.SemaphoreType.REGULAR,
            pltpu.SemaphoreType.DMA,
            pltpu.SemaphoreType.DMA,
        ],
        compiler_params=pltpu.CompilerParams(collective_id=0, has_side_effects=True),
    )(populations, pore_mask)


def solution(mesh):
    counts = tuple(mesh.shape[axis] for axis in ("gx", "gy", "gz"))
    placed = (P(None, "gx", "gy", "gz"), P("gx", "gy", "gz"))
    return jax.shard_map(
        functools.partial(body, counts),
        mesh=mesh,
        in_specs=placed,
        out_specs=P(None, "gx", "gy", "gz"),
        check_vma=False,
    )
```

```python
import functools

import jax
import jax.numpy as jnp
from jax import lax
from jax.experimental import pallas as pl
from jax.experimental.pallas import tpu as pltpu
from jax.sharding import PartitionSpec as P

LOADS = 3
MESH = pl.DeviceIdType.MESH

sound_sq = 2.0 / 3.0
relax_time = 0.8
pair_list = [(0, 0), (1, 1), (2, 2), (0, 1), (0, 2), (1, 2)]
triple_list = [
    (0, 0, 0),
    (1, 1, 1),
    (2, 2, 2),
    (0, 0, 1),
    (0, 0, 2),
    (1, 1, 0),
    (1, 1, 2),
    (2, 2, 0),
    (2, 2, 1),
    (0, 1, 2),
]
shell_weights = {
    (0, 0, 0): 1.0 / 12.0,
    (0, 0, 1): 1.0 / 12.0,
    (1, 1, 1): 1.0 / 27.0,
    (0, 0, 2): 2.0 / 135.0,
    (0, 2, 2): 1.0 / 432.0,
    (0, 0, 3): 1.0 / 1620.0,
}


def lattice():
    speeds = []
    weights = []
    for a in range(-3, 4):
        for b in range(-3, 4):
            for c in range(-3, 4):
                pattern = tuple(sorted((abs(a), abs(b), abs(c))))
                if pattern in shell_weights:
                    speeds.append((a, b, c))
                    weights.append(shell_weights[pattern])
    return speeds, weights


speeds, weights = lattice()
opposite = [speeds.index((-v[0], -v[1], -v[2])) for v in speeds]


def accumulate(total, factor, term):
    if factor == 0:
        return total
    if total is None:
        return term if factor == 1 else factor * term
    if factor == 1:
        return total + term
    if factor == -1:
        return total - term
    return total + factor * term


def collide(load):
    rest = speeds.index((0, 0, 0))
    pairs = [(k, opposite[k]) for k in range(len(speeds)) if k > opposite[k]]
    density = weights[rest] * load(rest)
    first = [None] * 3
    second = {ab: None for ab in pair_list}
    third = {abc: None for abc in triple_list}
    for shell in shell_weights:
        members = [(k, o) for k, o in pairs if tuple(sorted(map(abs, speeds[k]))) == shell]
        if not members:
            continue
        part0, part1 = None, [None] * 3
        part2 = {ab: None for ab in pair_list}
        part3 = {abc: None for abc in triple_list}
        for k, o in members:
            v = speeds[k]
            even = load(k) + load(o)
            odd = load(k) - load(o)
            part0 = accumulate(part0, 1, even)
            for a, b in pair_list:
                part2[a, b] = accumulate(part2[a, b], v[a] * v[b], even)
            for a in range(3):
                part1[a] = accumulate(part1[a], v[a], odd)
            for a, b, c in triple_list:
                part3[a, b, c] = accumulate(part3[a, b, c], v[a] * v[b] * v[c], odd)
        w = shell_weights[shell]
        density = accumulate(density, w, part0)
        for a in range(3):
            first[a] = accumulate(first[a], w, part1[a])
        for ab in pair_list:
            if part2[ab] is not None:
                second[ab] = accumulate(second[ab], w, part2[ab])
        for abc in triple_list:
            if part3[abc] is not None:
                third[abc] = accumulate(third[abc], w, part3[abc])

    inverse = 1.0 / density
    u = [first[a] * inverse for a in range(3)]
    relax = 1.0 - 1.0 / relax_time
    const = density
    linear = [first[a] * (1.0 / sound_sq) for a in range(3)]
    quad, cubic = {}, {}
    flux = {}
    for a, b in pair_list:
        flux[a, b] = first[a] * u[b]
        moment = second[a, b]
        if a == b:
            moment = moment - sound_sq * density
        scale = (1.0 if a == b else 2.0) / (2.0 * sound_sq**2)
        quad[a, b] = (scale * (1.0 - relax)) * flux[a, b] + (scale * relax) * moment
        if a == b:
            const = const - sound_sq * quad[a, b]
    for a, b, c in triple_list:
        moment = third[a, b, c]
        if a == b == c:
            moment = moment - (3.0 * sound_sq) * first[a]
        elif a == b:
            moment = moment - sound_sq * first[c]
        pair = (a, b) if (a, b) in flux else (b, a)
        scale = {1: 1.0, 2: 3.0, 3: 6.0}[len({a, b, c})] / (6.0 * sound_sq**3)
        cubic[a, b, c] = (scale * (1.0 - relax)) * (flux[pair] * u[c]) + (scale * relax) * moment
        if a == b == c:
            linear[a] = linear[a] - (3.0 * sound_sq) * cubic[a, b, c]
        elif a == b:
            linear[c] = linear[c] - sound_sq * cubic[a, b, c]

    return const, linear, quad, cubic


def half_sums(coefficients, k):
    const, linear, quad, cubic = coefficients
    v = speeds[k]
    even, odd = const, None
    for a, b in pair_list:
        even = accumulate(even, float(v[a] * v[b]), quad[a, b])
    for a in range(3):
        odd = accumulate(odd, float(v[a]), linear[a])
    for a, b, c in triple_list:
        odd = accumulate(odd, float(v[a] * v[b] * v[c]), cubic[a, b, c])
    return even, odd


def collided(load, pore, coefficients, k):
    o = opposite[k]
    if k == o:
        return jnp.where(pore, coefficients[0], load(o))
    even, odd = half_sums(coefficients, max(k, o))
    return jnp.where(pore, even + odd if k > o else even - odd, load(o))


def cut(speed, extent):
    if speed >= 0:
        return (0, extent - speed), (speed, extent), (extent - speed, extent), (0, speed)
    return (-speed, extent), (0, extent + speed), (0, -speed), (extent + speed, extent)


def merge_key(speed, rows, extent):
    return abs(speed) if 2 * rows <= extent else speed


def make_plan(nx, ny):
    sizes, slots, pieces = {}, {}, []
    for k, (cx, cy, cz) in enumerate(speeds):
        stay_from, stay_to, leave_from, leave_to = cut(cx, nx)
        own = []
        for source, land, dx in ((stay_from, stay_to, 0), (leave_from, leave_to, (cx > 0) - (cx < 0))):
            count = source[1] - source[0]
            if count == 0:
                continue
            where = {}
            for oy in (0, 1):
                for oz in (0, 1):
                    if (oy and not cy) or (oz and not cz) or (dx, oy, oz) == (0, 0, 0):
                        continue
                    key = (
                        dx,
                        oy,
                        oz,
                        cx,
                        merge_key(cy, abs(cy) if oy else ny - abs(cy), ny),
                        abs(cz) if oz else cz,
                    )
                    if key not in slots:
                        slots[key] = sizes.get((dx, oy, oz), 0)
                        sizes[dx, oy, oz] = slots[key] + count
                    where[oy, oz] = slots[key]
            own.append((source, land, dx, where))
        pieces.append(own)
    return sizes, pieces


def kind_of(step):
    return step[0], abs(step[1]), abs(step[2])


def neighbours(count):
    return (1,) if count == 2 else (1, -1)


def step_kernel(counts, pieces, messages, leave, arrive, pop_hbm, mask_hbm, out_ref, *scratch):
    send_ref, recv_ref, handed_ref, pop_ref, mask_ref = scratch[:5]
    send_sem, recv_sem, near_sem, handed_sem = scratch[5:]
    nx, ny, nz = out_ref.shape[1:]
    early = max(0, nx - max(abs(cx) for cx, _, cz in speeds if cz))
    ahead, behind = pl.ds(early, nx - early), pl.ds(0, early)
    ends = [len(speeds) * part // LOADS for part in range(LOADS + 1)]
    for start, stop in zip(ends, ends[1:]):
        planes = pl.ds(start, stop - start)
        pltpu.make_async_copy(pop_hbm.at[planes, ahead], pop_ref.at[planes, ahead], send_sem.at[0]).start()
    pltpu.make_async_copy(mask_hbm, mask_ref, send_sem.at[0]).start()
    load_rest = pltpu.make_async_copy(pop_hbm.at[:, behind], pop_ref.at[:, behind], send_sem.at[1])
    if early:
        load_rest.start()
    here = [lax.axis_index(axis) for axis in ("gx", "gy", "gz")]
    gx, length = here[0], counts[0]
    relay = length // 2
    first, last = gx == 0, gx == length - 1
    inner = (gx > 0) & (gx < length - 1)

    def target(step):
        return {
            axis: lax.rem(at + (s + count), count)
            for axis, at, s, count in zip(("gx", "gy", "gz"), here, step, counts)
            if s
        }

    def at_gx(step, index):
        return {**target((0,) + step[1:]), "gx": index}

    group = {dx: [step for step in messages if step[0] == dx] for dx in (1, 0, -1)}
    barrier = pltpu.get_barrier_semaphore()

    def signal(semaphore, device):
        pl.semaphore_signal(semaphore, inc=1, device_id=device, device_id_type=MESH)

    def greet(dx):
        for step in group[dx]:
            signal(barrier, target(step))

    greet(-1)
    pl.when(gx < length - 2)(lambda: greet(1))
    pl.when(gx < length - 1)(lambda: greet(0))

    @pl.when(last)
    def _():
        for step in group[-1]:
            signal(barrier, at_gx(step, relay))

    pl.when(gx == relay)(lambda: signal(barrier, {"gx": 0}))

    def remote(source, landing, send_semaphore, recv_semaphore, device):
        return pltpu.make_async_remote_copy(
            src_ref=source,
            dst_ref=landing,
            send_sem=send_semaphore,
            recv_sem=recv_semaphore,
            device_id=device,
            device_id_type=MESH,
        )

    def rows_of(ref, spans):
        spans = list(spans)
        return ref.at[pl.ds(spans[0][0], spans[-1][1] - spans[0][0])]

    def await_bytes(semaphore, ref):
        pltpu.make_async_copy(ref, ref, semaphore).wait()

    received = {dx: rows_of(recv_ref, (arrive[step] for step in group[dx])) for dx in group}
    received_rest = rows_of(recv_ref, (arrive[step] for step in group[0] + group[-1]))
    arrival_sem = {1: recv_sem.at[0], 0: recv_sem.at[1], -1: recv_sem.at[1]}
    span = arrive[group[-1][0]][0], arrive[group[-1][-1]][1]
    twice = recv_ref.at[pl.ds(0, 2 * (span[1] - span[0]))]
    away_sem = {1: send_sem.at[0], 0: send_sem.at[0], -1: send_sem.at[1]}
    first_handed = min(span[0] for name, span in leave.items() if name[0] == -1)
    to_hand = rows_of(send_ref, (leave[name] for name in leave if name[0] == -1))
    hand = remote(to_hand, handed_ref, send_sem.at[1], handed_sem, {"gx": relay})

    def depart(steps):
        for step in steps:
            remote(
                rows_of(send_ref, [leave[kind_of(step)]]),
                rows_of(recv_ref, [arrive[step]]),
                away_sem[step[0]],
                arrival_sem[step[0]],
                target(step),
            ).start()

    def forward(steps):
        for step in steps:
            start, stop = leave[kind_of(step)]
            remote(
                rows_of(handed_ref, [(start - first_handed, stop - first_handed)]),
                rows_of(recv_ref, [arrive[step]]),
                send_sem.at[1],
                arrival_sem[step[0]],
                at_gx(step, length - 1),
            ).start()

    await_bytes(send_sem.at[0], recv_ref.at[pl.ds(0, len(speeds) * (nx - early) + nx)])

    every_lane = slice(0, nz)
    loaders = [lambda j, row=row: pop_ref[j, row] for row in range(nx)]
    pores = [mask_ref[row] == 1 for row in range(nx)]
    coefficients = {}

    def place(k, row):
        if row not in coefficients:
            coefficients[row] = collide(loaders[row])
        cx, cy, cz = speeds[k]
        plane = collided(loaders[row], pores[row], coefficients[row], k)
        if cz:
            plane = pltpu.roll(plane, cz % nz, 1)
        y_stay, y_land, y_leave, y_wrap = (slice(*span) for span in cut(cy, ny))
        z_wrap = slice(*cut(cz, nz)[3])
        for source, land, dx, where in pieces[k]:
            if not source[0] <= row < source[1]:
                continue
            at = row - source[0]

            def slot(oy, oz):
                return leave[dx, oy, oz][0] + where[oy, oz] + at

            kept = plane[y_stay]
            if dx == 0:
                out_ref[k, land[0] + at, y_land, every_lane] = kept
            else:
                send_ref[slot(0, 0), y_land, every_lane] = kept
            if cy:
                moved = plane[y_leave]
                send_ref[slot(1, 0), y_wrap, every_lane] = moved
            if cz:
                send_ref[slot(0, 1), y_land, z_wrap] = kept[:, z_wrap]
            if cy and cz:
                send_ref[slot(1, 1), y_wrap, z_wrap] = moved[:, z_wrap]

    def place_all(dx, chosen=lambda cz: True):
        for row in reversed(range(nx)) if dx > 0 else range(nx):
            for k, (cx, _, cz) in enumerate(speeds):
                to = row + cx
                if (to >= nx) - (to < 0) == dx and chosen(cz):
                    place(k, row)

    at_first, at_last, at_relay = (jnp.where(gx == at, 1, 0) for at in (0, length - 1, relay))
    heard = len(messages) + at_relay * len(group[-1])
    heard -= at_first * (len(group[-1]) - 1) + at_last * (len(messages) - len(group[1]))
    place_all(1, lambda cz: cz != 0)
    pl.semaphore_wait(barrier, heard)
    depart([step for step in group[1] if step[2]])

    @pl.when(gx == length - 2)
    def _():
        for step in group[1]:
            signal(near_sem, target(step))

    if early:
        load_rest.wait()
    place_all(1, lambda cz: cz == 0)
    place_all(-1)
    place_all(0)
    depart([step for step in group[1] if not step[2]])
    pl.when(first)(lambda: hand.start())
    pl.when(inner)(lambda: depart(group[-1]))
    pl.when(last)(lambda: pl.semaphore_wait(near_sem, len(group[-1])))
    depart(group[0])
    pl.when(last)(lambda: depart(group[-1]))

    @pl.when(gx == relay)
    def _():
        hand.wait_recv()
        forward(group[-1])

    def came_by(step, speed):
        return step == 0 or step * speed > 0

    def block(span, rows, lanes):
        return (slice(*span), slice(*rows), slice(*lanes))

    def unpack(dx):
        for step in group[dx]:
            _, sy, sz = step
            for k, (cx, cy, cz) in enumerate(speeds):
                if (sy and not cy) or (sz and not cz):
                    continue
                if counts[1] != 2 and not came_by(sy, cy):
                    continue
                if counts[2] != 2 and not came_by(sz, cz):
                    continue
                _, y_land, _, y_wrap = cut(cy, ny)
                rows = y_wrap if sy else y_land
                lanes = cut(cz, nz)[3 if sz else 1]
                for source, land, piece_dx, where in pieces[k]:
                    if piece_dx != dx:
                        continue
                    at = arrive[step][0] + where[abs(sy), abs(sz)]
                    span = (at, at + source[1] - source[0])
                    out_ref[(k,) + block(land, rows, lanes)] = recv_ref[block(span, rows, lanes)]

    await_bytes(recv_sem.at[1], received_rest)
    unpack(0)
    unpack(-1)
    await_bytes(send_sem.at[0], rows_of(recv_ref, (arrive[step] for step in group[1] + group[0])))
    pl.when(first)(lambda: hand.wait_send())
    pl.when((gx > 0) & (gx != relay))(lambda: await_bytes(send_sem.at[1], received[-1]))
    pl.when(gx == relay)(lambda: await_bytes(send_sem.at[1], twice))
    await_bytes(recv_sem.at[0], received[1])
    unpack(1)


def lay_out(keys, size):
    spans, start = {}, 0
    for key in keys:
        spans[key] = (start, start + size(key))
        start += size(key)
    return spans, start


def body(counts, populations, pore_mask):
    nx, ny = populations.shape[1:3]
    sizes, pieces = make_plan(nx, ny)
    messages = []
    for dx, oz, oy in [(dx, oz, oy) for dx in (1, 0, -1) for oz, oy in ((1, 0), (1, 1), (0, 0), (0, 1))]:
        if (dx, oz, oy) == (0, 0, 0):
            continue
        for sy in neighbours(counts[1]) if oy else (0,):
            for sz in neighbours(counts[2]) if oz else (0,):
                messages.append((dx, sy, sz))
    kinds = list(dict.fromkeys(kind_of(step) for step in messages))
    leave, leaving = lay_out(kinds, lambda kind: sizes[kind])
    arrive, arriving = lay_out(messages, lambda step: sizes[kind_of(step)])
    handed = sum(sizes[kind] for kind in kinds if kind[0] == -1)
    rows = lambda count: pltpu.VMEM((count, ny, populations.shape[3]), jnp.float32)
    return pl.pallas_call(
        functools.partial(step_kernel, counts, pieces, messages, leave, arrive),
        out_shape=pltpu.VMEM(populations.shape, populations.dtype),
        in_specs=[pl.BlockSpec(memory_space=pl.ANY)] * 2,
        out_specs=pl.BlockSpec(memory_space=pltpu.VMEM),
        scratch_shapes=[
            rows(leaving),
            rows(max(arriving, (len(speeds) + 1) * nx)),
            rows(handed),
            pltpu.VMEM(populations.shape, populations.dtype),
            pltpu.VMEM(pore_mask.shape, pore_mask.dtype),
            pltpu.SemaphoreType.DMA((2,)),
            pltpu.SemaphoreType.DMA((2,)),
            pltpu.SemaphoreType.REGULAR,
            pltpu.SemaphoreType.DMA,
        ],
        compiler_params=pltpu.CompilerParams(collective_id=0, has_side_effects=True),
    )(populations, pore_mask)


def solution(mesh):
    counts = tuple(mesh.shape[axis] for axis in ("gx", "gy", "gz"))
    placed = (P(None, "gx", "gy", "gz"), P("gx", "gy", "gz"))
    return jax.shard_map(
        functools.partial(body, counts),
        mesh=mesh,
        in_specs=placed,
        out_specs=P(None, "gx", "gy", "gz"),
        check_vma=False,
    )
```

```python
import functools

import jax
import jax.numpy as jnp
from jax import lax
from jax.experimental import pallas as pl
from jax.experimental.pallas import tpu as pltpu
from jax.sharding import PartitionSpec as P

LOADS = 6
MESH = pl.DeviceIdType.MESH

sound_sq = 2.0 / 3.0
relax_time = 0.8
pair_list = [(0, 0), (1, 1), (2, 2), (0, 1), (0, 2), (1, 2)]
triple_list = [
    (0, 0, 0),
    (1, 1, 1),
    (2, 2, 2),
    (0, 0, 1),
    (0, 0, 2),
    (1, 1, 0),
    (1, 1, 2),
    (2, 2, 0),
    (2, 2, 1),
    (0, 1, 2),
]
shell_weights = {
    (0, 0, 0): 1.0 / 12.0,
    (0, 0, 1): 1.0 / 12.0,
    (1, 1, 1): 1.0 / 27.0,
    (0, 0, 2): 2.0 / 135.0,
    (0, 2, 2): 1.0 / 432.0,
    (0, 0, 3): 1.0 / 1620.0,
}


def lattice():
    speeds = []
    weights = []
    for a in range(-3, 4):
        for b in range(-3, 4):
            for c in range(-3, 4):
                pattern = tuple(sorted((abs(a), abs(b), abs(c))))
                if pattern in shell_weights:
                    speeds.append((a, b, c))
                    weights.append(shell_weights[pattern])
    return speeds, weights


speeds, weights = lattice()
opposite = [speeds.index((-v[0], -v[1], -v[2])) for v in speeds]


def accumulate(total, factor, term):
    if factor == 0:
        return total
    if total is None:
        return term if factor == 1 else factor * term
    if factor == 1:
        return total + term
    if factor == -1:
        return total - term
    return total + factor * term


def collide(load):
    rest = speeds.index((0, 0, 0))
    pairs = [(k, opposite[k]) for k in range(len(speeds)) if k > opposite[k]]
    density = weights[rest] * load(rest)
    first = [None] * 3
    second = {ab: None for ab in pair_list}
    third = {abc: None for abc in triple_list}
    for shell in shell_weights:
        members = [(k, o) for k, o in pairs if tuple(sorted(map(abs, speeds[k]))) == shell]
        if not members:
            continue
        part0, part1 = None, [None] * 3
        part2 = {ab: None for ab in pair_list}
        part3 = {abc: None for abc in triple_list}
        for k, o in members:
            v = speeds[k]
            even = load(k) + load(o)
            odd = load(k) - load(o)
            part0 = accumulate(part0, 1, even)
            for a, b in pair_list:
                part2[a, b] = accumulate(part2[a, b], v[a] * v[b], even)
            for a in range(3):
                part1[a] = accumulate(part1[a], v[a], odd)
            for a, b, c in triple_list:
                part3[a, b, c] = accumulate(part3[a, b, c], v[a] * v[b] * v[c], odd)
        w = shell_weights[shell]
        density = accumulate(density, w, part0)
        for a in range(3):
            first[a] = accumulate(first[a], w, part1[a])
        for ab in pair_list:
            if part2[ab] is not None:
                second[ab] = accumulate(second[ab], w, part2[ab])
        for abc in triple_list:
            if part3[abc] is not None:
                third[abc] = accumulate(third[abc], w, part3[abc])

    inverse = 1.0 / density
    u = [first[a] * inverse for a in range(3)]
    relax = 1.0 - 1.0 / relax_time
    const = density
    linear = [first[a] * (1.0 / sound_sq) for a in range(3)]
    quad, cubic = {}, {}
    flux = {}
    for a, b in pair_list:
        flux[a, b] = first[a] * u[b]
        moment = second[a, b]
        if a == b:
            moment = moment - sound_sq * density
        scale = (1.0 if a == b else 2.0) / (2.0 * sound_sq**2)
        quad[a, b] = (scale * (1.0 - relax)) * flux[a, b] + (scale * relax) * moment
        if a == b:
            const = const - sound_sq * quad[a, b]
    for a, b, c in triple_list:
        moment = third[a, b, c]
        if a == b == c:
            moment = moment - (3.0 * sound_sq) * first[a]
        elif a == b:
            moment = moment - sound_sq * first[c]
        pair = (a, b) if (a, b) in flux else (b, a)
        scale = {1: 1.0, 2: 3.0, 3: 6.0}[len({a, b, c})] / (6.0 * sound_sq**3)
        cubic[a, b, c] = (scale * (1.0 - relax)) * (flux[pair] * u[c]) + (scale * relax) * moment
        if a == b == c:
            linear[a] = linear[a] - (3.0 * sound_sq) * cubic[a, b, c]
        elif a == b:
            linear[c] = linear[c] - sound_sq * cubic[a, b, c]

    return const, linear, quad, cubic


def half_sums(coefficients, k):
    const, linear, quad, cubic = coefficients
    v = speeds[k]
    even, odd = const, None
    for a, b in pair_list:
        even = accumulate(even, float(v[a] * v[b]), quad[a, b])
    for a in range(3):
        odd = accumulate(odd, float(v[a]), linear[a])
    for a, b, c in triple_list:
        odd = accumulate(odd, float(v[a] * v[b] * v[c]), cubic[a, b, c])
    return even, odd


def collided(load, pore, coefficients, k):
    o = opposite[k]
    if k == o:
        return jnp.where(pore, coefficients[0], load(o))
    even, odd = half_sums(coefficients, max(k, o))
    return jnp.where(pore, even + odd if k > o else even - odd, load(o))


def cut(speed, extent):
    if speed >= 0:
        return (0, extent - speed), (speed, extent), (extent - speed, extent), (0, speed)
    return (-speed, extent), (0, extent + speed), (0, -speed), (extent + speed, extent)


def merge_key(speed, rows, extent):
    return abs(speed) if 2 * rows <= extent else speed


def make_plan(nx, ny):
    sizes, slots, pieces = {}, {}, []
    for k, (cx, cy, cz) in enumerate(speeds):
        stay_from, stay_to, leave_from, leave_to = cut(cx, nx)
        own = []
        for source, land, dx in ((stay_from, stay_to, 0), (leave_from, leave_to, (cx > 0) - (cx < 0))):
            count = source[1] - source[0]
            if count == 0:
                continue
            where = {}
            for oy in (0, 1):
                for oz in (0, 1):
                    if (oy and not cy) or (oz and not cz) or (dx, oy, oz) == (0, 0, 0):
                        continue
                    key = (
                        dx,
                        oy,
                        oz,
                        cx,
                        merge_key(cy, abs(cy) if oy else ny - abs(cy), ny),
                        abs(cz) if oz else cz,
                    )
                    if key not in slots:
                        slots[key] = sizes.get((dx, oy, oz), 0)
                        sizes[dx, oy, oz] = slots[key] + count
                    where[oy, oz] = slots[key]
            own.append((source, land, dx, where))
        pieces.append(own)
    return sizes, pieces


def kind_of(step):
    return step[0], abs(step[1]), abs(step[2])


def neighbours(count):
    return (1,) if count == 2 else (1, -1)


def step_kernel(counts, pieces, messages, leave, arrive, pop_hbm, mask_hbm, out_ref, *scratch):
    send_ref, recv_ref, handed_ref, pop_ref, mask_ref = scratch[:5]
    send_sem, recv_sem, near_sem, handed_sem = scratch[5:]
    nx, ny, nz = out_ref.shape[1:]
    early = max(0, nx - max(abs(cx) for cx, _, cz in speeds if cz))
    ahead, behind = pl.ds(early, nx - early), pl.ds(0, early)
    ends = [len(speeds) * part // LOADS for part in range(LOADS + 1)]
    for start, stop in zip(ends, ends[1:]):
        planes = pl.ds(start, stop - start)
        pltpu.make_async_copy(pop_hbm.at[planes, ahead], pop_ref.at[planes, ahead], send_sem.at[0]).start()
    pltpu.make_async_copy(mask_hbm, mask_ref, send_sem.at[0]).start()
    load_rest = pltpu.make_async_copy(pop_hbm.at[:, behind], pop_ref.at[:, behind], send_sem.at[1])
    if early:
        load_rest.start()
    here = [lax.axis_index(axis) for axis in ("gx", "gy", "gz")]
    gx, length = here[0], counts[0]
    relay = length // 2
    first, last = gx == 0, gx == length - 1
    inner = (gx > 0) & (gx < length - 1)

    def target(step):
        return {
            axis: lax.rem(at + (s + count), count)
            for axis, at, s, count in zip(("gx", "gy", "gz"), here, step, counts)
            if s
        }

    def at_gx(step, index):
        return {**target((0,) + step[1:]), "gx": index}

    group = {dx: [step for step in messages if step[0] == dx] for dx in (1, 0, -1)}
    barrier = pltpu.get_barrier_semaphore()

    def signal(semaphore, device):
        pl.semaphore_signal(semaphore, inc=1, device_id=device, device_id_type=MESH)

    def greet(dx):
        for step in group[dx]:
            signal(barrier, target(step))

    greet(-1)
    pl.when(gx < length - 2)(lambda: greet(1))
    pl.when(gx < length - 1)(lambda: greet(0))

    @pl.when(last)
    def _():
        for step in group[-1]:
            signal(barrier, at_gx(step, relay))

    pl.when(gx == relay)(lambda: signal(barrier, {"gx": 0}))

    def remote(source, landing, send_semaphore, recv_semaphore, device):
        return pltpu.make_async_remote_copy(
            src_ref=source,
            dst_ref=landing,
            send_sem=send_semaphore,
            recv_sem=recv_semaphore,
            device_id=device,
            device_id_type=MESH,
        )

    def rows_of(ref, spans):
        spans = list(spans)
        return ref.at[pl.ds(spans[0][0], spans[-1][1] - spans[0][0])]

    def await_bytes(semaphore, ref):
        pltpu.make_async_copy(ref, ref, semaphore).wait()

    received = {dx: rows_of(recv_ref, (arrive[step] for step in group[dx])) for dx in group}
    received_rest = rows_of(recv_ref, (arrive[step] for step in group[0] + group[-1]))
    arrival_sem = {1: recv_sem.at[0], 0: recv_sem.at[1], -1: recv_sem.at[1]}
    span = arrive[group[-1][0]][0], arrive[group[-1][-1]][1]
    twice = recv_ref.at[pl.ds(0, 2 * (span[1] - span[0]))]
    away_sem = {1: send_sem.at[0], 0: send_sem.at[0], -1: send_sem.at[1]}
    first_handed = min(span[0] for name, span in leave.items() if name[0] == -1)
    to_hand = rows_of(send_ref, (leave[name] for name in leave if name[0] == -1))
    hand = remote(to_hand, handed_ref, send_sem.at[1], handed_sem, {"gx": relay})

    def depart(steps):
        for step in steps:
            remote(
                rows_of(send_ref, [leave[kind_of(step)]]),
                rows_of(recv_ref, [arrive[step]]),
                away_sem[step[0]],
                arrival_sem[step[0]],
                target(step),
            ).start()

    def forward(steps):
        for step in steps:
            start, stop = leave[kind_of(step)]
            remote(
                rows_of(handed_ref, [(start - first_handed, stop - first_handed)]),
                rows_of(recv_ref, [arrive[step]]),
                send_sem.at[1],
                arrival_sem[step[0]],
                at_gx(step, length - 1),
            ).start()

    await_bytes(send_sem.at[0], recv_ref.at[pl.ds(0, len(speeds) * (nx - early) + nx)])

    every_lane = slice(0, nz)
    loaders = [lambda j, row=row: pop_ref[j, row] for row in range(nx)]
    pores = [mask_ref[row] == 1 for row in range(nx)]
    coefficients = {}

    def place(k, row):
        if row not in coefficients:
            coefficients[row] = collide(loaders[row])
        cx, cy, cz = speeds[k]
        plane = collided(loaders[row], pores[row], coefficients[row], k)
        if cz:
            plane = pltpu.roll(plane, cz % nz, 1)
        y_stay, y_land, y_leave, y_wrap = (slice(*span) for span in cut(cy, ny))
        z_wrap = slice(*cut(cz, nz)[3])
        for source, land, dx, where in pieces[k]:
            if not source[0] <= row < source[1]:
                continue
            at = row - source[0]

            def slot(oy, oz):
                return leave[dx, oy, oz][0] + where[oy, oz] + at

            kept = plane[y_stay]
            if dx == 0:
                out_ref[k, land[0] + at, y_land, every_lane] = kept
            else:
                send_ref[slot(0, 0), y_land, every_lane] = kept
            if cy:
                moved = plane[y_leave]
                send_ref[slot(1, 0), y_wrap, every_lane] = moved
            if cz:
                send_ref[slot(0, 1), y_land, z_wrap] = kept[:, z_wrap]
            if cy and cz:
                send_ref[slot(1, 1), y_wrap, z_wrap] = moved[:, z_wrap]

    def place_all(dx, chosen=lambda cz: True):
        for row in reversed(range(nx)) if dx > 0 else range(nx):
            for k, (cx, _, cz) in enumerate(speeds):
                to = row + cx
                if (to >= nx) - (to < 0) == dx and chosen(cz):
                    place(k, row)

    at_first, at_last, at_relay = (jnp.where(gx == at, 1, 0) for at in (0, length - 1, relay))
    heard = len(messages) + at_relay * len(group[-1])
    heard -= at_first * (len(group[-1]) - 1) + at_last * (len(messages) - len(group[1]))
    place_all(1, lambda cz: cz != 0)
    pl.semaphore_wait(barrier, heard)
    depart([step for step in group[1] if step[2]])

    @pl.when(gx == length - 2)
    def _():
        for step in group[1]:
            signal(near_sem, target(step))

    if early:
        load_rest.wait()
    place_all(1, lambda cz: cz == 0)
    place_all(-1)
    place_all(0)
    depart([step for step in group[1] if not step[2]])
    pl.when(first)(lambda: hand.start())
    pl.when(inner)(lambda: depart(group[-1]))
    pl.when(last)(lambda: pl.semaphore_wait(near_sem, len(group[-1])))
    depart(group[0])
    pl.when(last)(lambda: depart(group[-1]))

    @pl.when(gx == relay)
    def _():
        hand.wait_recv()
        forward(group[-1])

    def came_by(step, speed):
        return step == 0 or step * speed > 0

    def block(span, rows, lanes):
        return (slice(*span), slice(*rows), slice(*lanes))

    def unpack(dx):
        for step in group[dx]:
            _, sy, sz = step
            for k, (cx, cy, cz) in enumerate(speeds):
                if (sy and not cy) or (sz and not cz):
                    continue
                if counts[1] != 2 and not came_by(sy, cy):
                    continue
                if counts[2] != 2 and not came_by(sz, cz):
                    continue
                _, y_land, _, y_wrap = cut(cy, ny)
                rows = y_wrap if sy else y_land
                lanes = cut(cz, nz)[3 if sz else 1]
                for source, land, piece_dx, where in pieces[k]:
                    if piece_dx != dx:
                        continue
                    at = arrive[step][0] + where[abs(sy), abs(sz)]
                    span = (at, at + source[1] - source[0])
                    out_ref[(k,) + block(land, rows, lanes)] = recv_ref[block(span, rows, lanes)]

    await_bytes(recv_sem.at[1], received_rest)
    unpack(0)
    unpack(-1)
    await_bytes(send_sem.at[0], rows_of(recv_ref, (arrive[step] for step in group[1] + group[0])))
    pl.when(first)(lambda: hand.wait_send())
    pl.when((gx > 0) & (gx != relay))(lambda: await_bytes(send_sem.at[1], received[-1]))
    pl.when(gx == relay)(lambda: await_bytes(send_sem.at[1], twice))
    await_bytes(recv_sem.at[0], received[1])
    unpack(1)


def lay_out(keys, size):
    spans, start = {}, 0
    for key in keys:
        spans[key] = (start, start + size(key))
        start += size(key)
    return spans, start


def body(counts, populations, pore_mask):
    nx, ny = populations.shape[1:3]
    sizes, pieces = make_plan(nx, ny)
    messages = []
    for dx, oz, oy in [(dx, oz, oy) for dx in (1, 0, -1) for oz, oy in ((1, 0), (1, 1), (0, 0), (0, 1))]:
        if (dx, oz, oy) == (0, 0, 0):
            continue
        for sy in neighbours(counts[1]) if oy else (0,):
            for sz in neighbours(counts[2]) if oz else (0,):
                messages.append((dx, sy, sz))
    kinds = list(dict.fromkeys(kind_of(step) for step in messages))
    leave, leaving = lay_out(kinds, lambda kind: sizes[kind])
    arrive, arriving = lay_out(messages, lambda step: sizes[kind_of(step)])
    handed = sum(sizes[kind] for kind in kinds if kind[0] == -1)
    rows = lambda count: pltpu.VMEM((count, ny, populations.shape[3]), jnp.float32)
    return pl.pallas_call(
        functools.partial(step_kernel, counts, pieces, messages, leave, arrive),
        out_shape=pltpu.VMEM(populations.shape, populations.dtype),
        in_specs=[pl.BlockSpec(memory_space=pl.ANY)] * 2,
        out_specs=pl.BlockSpec(memory_space=pltpu.VMEM),
        scratch_shapes=[
            rows(leaving),
            rows(max(arriving, (len(speeds) + 1) * nx)),
            rows(handed),
            pltpu.VMEM(populations.shape, populations.dtype),
            pltpu.VMEM(pore_mask.shape, pore_mask.dtype),
            pltpu.SemaphoreType.DMA((2,)),
            pltpu.SemaphoreType.DMA((2,)),
            pltpu.SemaphoreType.REGULAR,
            pltpu.SemaphoreType.DMA,
        ],
        compiler_params=pltpu.CompilerParams(collective_id=0, has_side_effects=True),
    )(populations, pore_mask)


def solution(mesh):
    counts = tuple(mesh.shape[axis] for axis in ("gx", "gy", "gz"))
    placed = (P(None, "gx", "gy", "gz"), P("gx", "gy", "gz"))
    return jax.shard_map(
        functools.partial(body, counts),
        mesh=mesh,
        in_specs=placed,
        out_specs=P(None, "gx", "gy", "gz"),
        check_vma=False,
    )
```
